32 devices in a mesh: kpt: 8 (over z, core), row: 4 (over y, x).
Axes of the slice: x: 2, y: 2, z: 4, core: 2. Of those that a mesh axis runs over, the one named last changes fastest.
Arguments:
- occ_orbitals: bfloat16 [32, 2048, 128], P('kpt', 'row'), may hold values from -0.5 to 0.5
- virt_orbitals: bfloat16 [32, 2048, 256], P('kpt', 'row'), may hold values from -0.375 to 0.375
- occ_gap: bfloat16 [32, 128], P('kpt'), may hold values from 0.049804688 to 3
- virt_gap: bfloat16 [32, 256], P('kpt'), may hold values from 0.049804688 to 3
- partner: int32 [3, 32], replicated, may hold values from 0 to 31, as said below
Outputs:
- chi: float32 [3, 4, 2048, 2048], P(None, None, 'row', 'kpt')
The draws below stay inside these ranges and needn't reach their ends.
Inputs may be any that keep to these rules, and one draw needn't show every extreme that they name: For each transfer q there is a shift s_q of 0 to 4 with partner[q, k] = (k - s_q) mod 32 for every k; the shifts of different transfers differ, and some transfer has s_q = 4.
All inputs are finite; a program needn't handle non-finite values.
Results may differ from the reference program's by a relative error of at most 0.0003.
Values may be sent and summed in bfloat16 or wider, within the bound.
A program may use at most 384 MiB of HBM per device.

```python
import math
import jax
import jax.numpy as jnp
from jax import lax

NP = 2048
NOCC = 128
NV = 256
NTAU = 4
QWIN = 3
K_DEV = 4
K = 32


def draw_partner(key, part):
    others = jax.random.permutation(jax.random.fold_in(key, 7), jnp.arange(K_DEV, dtype=jnp.int32))[:QWIN - 1].astype(jnp.int32)
    shift_values = jnp.concatenate([jnp.full((1,), K_DEV, jnp.int32), others])
    shift_values = jax.random.permutation(jax.random.fold_in(key, 11), shift_values).astype(jnp.int32)
    momentum_ids = jnp.arange(K, dtype=jnp.int32)
    return ((momentum_ids[None, :] - shift_values[:, None]) % K).astype(jnp.int32)


def levels(rng, extent, pieces, least, high):
    def one(dim, blocks):
        steps = jax.random.uniform(jax.random.fold_in(jax.random.fold_in(rng, 6), dim), (blocks,), jnp.float32, least / len(pieces), high / len(pieces))
        return jnp.repeat(jnp.exp(steps), extent[dim] // blocks).reshape((-1,) + (1,) * (len(extent) - dim - 1))

    gain = one(*pieces[0])
    for cut in pieces[1:]:
        gain = gain * one(*cut)
    return gain


def normal_values(own_key, extent, deviation, most, pieces=(), kind=jnp.bfloat16):
    drawn = jax.random.normal(own_key, extent, jnp.float32) * deviation
    if len(pieces) > 0:
        drawn = levels(own_key, extent, pieces, -0.22, 0.18) * drawn
    return jnp.clip(drawn, min=-most, max=most).astype(kind)


def setup_inputs(seed: int = 0) -> dict:
    seeds = jax.random.split(jax.random.key(seed), 6)
    occ_orbitals = normal_values(seeds[0], (K, NP, NOCC), NOCC ** -0.5, 0.5, ((0, 8), (1, 4)))
    virt_orbitals = normal_values(seeds[1], (K, NP, NV), NV ** -0.5, 0.375, ((0, 8), (1, 4)))
    occ_gap = jnp.clip(jnp.exp(math.log(3.0) - 4.0982585 * jax.random.uniform(seeds[2], (K, NOCC), jnp.float32) ** levels(seeds[2], (K, NOCC), ((0, 8),), -0.2, 0.2)), 0.049804688, 3.0).astype(jnp.bfloat16)
    virt_gap = jnp.clip(jnp.exp(math.log(3.0) - 4.0982585 * jax.random.uniform(seeds[3], (K, NV), jnp.float32) ** levels(seeds[3], (K, NV), ((0, 8),), -0.2, 0.2)), 0.049804688, 3.0).astype(jnp.bfloat16)
    partner = draw_partner(jax.random.fold_in(seeds[5], 71), 0)
    return dict(occ_orbitals=occ_orbitals, virt_orbitals=virt_orbitals, occ_gap=occ_gap, virt_gap=virt_gap, partner=partner)


def reference(occ_orbitals, virt_orbitals, occ_gap, virt_gap, partner):
    tau_values = 0.25 * 2.0 ** jnp.arange(NTAU, dtype=jnp.float32)
    momentum_ids = jnp.arange(K, dtype=jnp.int32)
    results = []
    for step_index in range(NTAU):
        moment = tau_values[step_index]

        def accumulate(running, momentum):
            occ_rows = occ_orbitals[momentum]
            occ_factor = jnp.exp(-occ_gap[momentum].astype(jnp.float32) * moment)
            occ_panel = (occ_rows.astype(jnp.float32) * occ_factor[None, :]).astype(jnp.bfloat16)
            occ_green = jnp.dot(occ_panel, occ_rows.T, preferred_element_type=jnp.float32)
            updated = []
            for transfer in range(QWIN):
                partner_id = partner[transfer, momentum]
                virt_rows = virt_orbitals[partner_id]
                virt_factor = jnp.exp(-virt_gap[partner_id].astype(jnp.float32) * moment)
                virt_panel = (virt_rows.astype(jnp.float32) * virt_factor[None, :]).astype(jnp.bfloat16)
                virt_green = jnp.dot(virt_panel, virt_rows.T, preferred_element_type=jnp.float32)
                updated.append(running[transfer] + occ_green * virt_green)
            return jnp.stack(updated), None

        running, _ = lax.scan(accumulate, jnp.zeros((QWIN, NP, NP), jnp.float32), momentum_ids)
        results.append(running)
    return jnp.stack(results, axis=1)
```

```python
import functools

import jax
import jax.numpy as jnp
from jax import lax
from jax.experimental import pallas as pl
from jax.experimental.pallas import tpu as pltpu
from jax.sharding import PartitionSpec as P

NTAU = 4
PAD = 16
SUB = 32
PIECES = 4


def kernel(nk, nr, per, occ_ref, virt_ref, gap_ref, partner_ref, chi, rows, cols, gaps, og, vg, last_og, last_vg,
           local_sem, row_recv, flow_send, sib_send, gap_recv, gap_flow, gap_sib, col_recv, col_send):
    K = nk * per
    npts, nocc = occ_ref.shape[1], occ_ref.shape[2]
    nall = rows.shape[2]
    ncol = cols.shape[1]
    width = ncol // PIECES
    transfers = partner_ref.shape[0]
    j = lax.axis_index("kpt")
    i = lax.axis_index("row")
    c, s = j // 2, j % 2
    nc = nk // 2
    cpr = nk // nr
    root = j // cpr
    off = (j % cpr) * ncol
    span = 2 * per

    def place(index):
        return jnp.where(index % 2 == 0, index // 2, nr - 1 - index // 2)

    def at_place(p):
        return jnp.where(p < nr // 2, 2 * p, 2 * (nr - 1 - p) + 1)

    me, top = place(i), place(root)
    ahead, behind = at_place((me + 1) % nr), at_place((me + nr - 1) % nr)
    dist_a, dist_b = (me - top + nr) % nr, (top - me + nr) % nr
    is_root = i == root
    up = s == 0
    has_next = jnp.where(up, c + 1 < nc, c > 0)
    has_prev = jnp.where(up, c > 0, c + 1 < nc)
    sib = j + 1 - 2 * s
    onward = j + 2 - 4 * s
    before = j - 2 + 4 * s

    def local_rows(a):
        m = j * per + a
        return (pltpu.make_async_copy(occ_ref.at[a], rows.at[m, :, pl.ds(0, nocc)], local_sem.at[a, 0]),
                pltpu.make_async_copy(virt_ref.at[a], rows.at[m, :, pl.ds(nocc, nall - nocc)], local_sem.at[a, 1]))

    local_gap = pltpu.make_async_copy(gap_ref, gaps.at[j], gap_recv.at[j])
    local_gap.start()
    for a in range(per):
        for copy in local_rows(a):
            copy.start()

    barrier = pltpu.get_barrier_semaphore()

    def greet(device):
        pl.semaphore_signal(barrier, inc=1, device_id=device, device_id_type=pl.DeviceIdType.MESH)

    greet((sib, i))
    greet((j, ahead))
    greet((j, behind))

    @pl.when(has_next)
    def _():
        greet((onward, i))

    @pl.when(has_prev)
    def _():
        greet((before, i))

    pl.semaphore_wait(barrier, 3 + has_next.astype(jnp.int32) + has_prev.astype(jnp.int32))

    def remote(src, dst, send, recv, device):
        return pltpu.make_async_remote_copy(src_ref=src, dst_ref=dst, send_sem=send, recv_sem=recv,
                                            device_id=device, device_id_type=pl.DeviceIdType.MESH)

    def row_flow(m):
        return remote(rows.at[m], rows.at[m], flow_send.at[m], row_recv.at[m], (onward, i))

    def row_sib(m):
        return remote(rows.at[m], rows.at[m], sib_send.at[m], row_recv.at[m], (sib, i))

    def gap_on(b):
        return remote(gaps.at[b], gaps.at[b], gap_flow.at[b], gap_recv.at[b], (onward, i))

    def gap_over(b):
        return remote(gaps.at[b], gaps.at[b], gap_sib.at[b], gap_recv.at[b], (sib, i))

    def part(p):
        return pl.ds(p * width, width)

    def source(m, p):
        return rows.at[m, pl.ds(pl.multiple_of(off + p * width, width), width)]

    def col_copy(m, p, device, from_root):
        src = source(m, p) if from_root else cols.at[m, part(p)]
        return remote(src, cols.at[m, part(p)], col_send.at[m, p], col_recv.at[m, p], (j, device))

    def root_copy(m, p):
        return pltpu.make_async_copy(source(m, p), cols.at[m, part(p)], col_recv.at[m, p])

    def wait_row(m):
        pltpu.make_async_copy(rows.at[m], rows.at[m], row_recv.at[m]).wait()

    def wait_gap(b):
        pltpu.make_async_copy(gaps.at[b], gaps.at[b], gap_recv.at[b]).wait()

    def wait_col(m, p):
        pltpu.make_async_copy(cols.at[m, part(p)], cols.at[m, part(p)], col_recv.at[m, p]).wait()

    ways = tuple((p, (dist_a, dist_b)[p % 2], (ahead, behind)[p % 2]) for p in range(PIECES))

    def root_send(m, start):
        @pl.when(is_root)
        def _():
            for p, _, device in ways:
                copy = col_copy(m, p, device, True)
                copy.start() if start else copy.wait_send()
                if start:
                    root_copy(m, p).start()

    def arrivals(n):
        h, idx = n // span, n % span
        low, high = c - h, c + h
        first = low * span + idx
        second = high * span + (idx + per) % span
        flow_ok = jnp.where(up, low >= 0, high < nc)
        other_ok = (h > 0) & jnp.where(up, high < nc, low >= 0)
        return h, idx, jnp.where(up, first, second), flow_ok, jnp.where(up, second, first), other_ok

    def row_stage(n, start):
        h, idx, fm, flow_ok, om, other_ok = arrivals(n)
        own = (h == 0) & (idx < per)
        lead = idx % per == 0

        def go(copy):
            copy.start() if start else copy.wait_send()

        @pl.when(flow_ok)
        def _():
            if start:
                @pl.when(own)
                def _():
                    for copy in local_rows(idx % per):
                        copy.wait()

                @pl.when(jnp.logical_not(own))
                def _():
                    wait_row(fm)

                @pl.when(lead)
                def _():
                    wait_gap(fm // per)

            @pl.when(has_next)
            def _():
                go(row_flow(fm))

                @pl.when(lead)
                def _():
                    go(gap_on(fm // per))

            @pl.when((h > 0) | own)
            def _():
                go(row_sib(fm))

                @pl.when(lead)
                def _():
                    go(gap_over(fm // per))

            root_send(fm, start)

        @pl.when(other_ok)
        def _():
            if start:
                wait_row(om)

                @pl.when(lead)
                def _():
                    wait_gap(om // per)
            root_send(om, start)

    def col_stage(n, start, p, dist, device):
        _, _, fm, flow_ok, om, other_ok = arrivals(n)
        for m, ok in ((fm, flow_ok), (om, other_ok)):
            @pl.when(ok)
            def _():
                if start:
                    wait_col(m, p)

                @pl.when((dist > 0) & (dist < nr - 1))
                def _():
                    copy = col_copy(m, p, device, False)
                    copy.start() if start else copy.wait_send()

    contract = (((1,), (1,)), ((), ()))

    def factors(b, t):
        moment = jnp.where(t == 0, 0.25, jnp.where(t == 1, 0.5, jnp.where(t == 2, 1.0, 2.0))).astype(jnp.float32)
        return jnp.exp(-gaps[b].astype(jnp.float32) * moment)

    def product(k, scale, low, size):
        panel = (rows[k, :, pl.ds(low, size)].astype(jnp.float32) * scale[:, low:low + size]).astype(jnp.bfloat16)
        return lax.dot_general(panel, cols[k, :, pl.ds(low, size)], contract, preferred_element_type=jnp.float32)

    def occ_green(k, scale):
        return product(k, scale, 0, nocc)

    def virt_green(k, scale):
        return product(k, scale, nocc, nall - nocc)

    def add(t, ks, base, held, occ_at, virt_at):
        slots = []
        for k in ks:
            for q in range(transfers):
                d = partner_ref[q, k] - base
                slots.append(jnp.minimum(jnp.where(d < 0, d + K, d), held - 1))

        def piece(p, inner):
            here = pl.ds(pl.multiple_of(p * SUB, SUB), SUB)
            sums = [chi[q, t, here, :] for q in range(transfers)]
            for a in range(len(ks)):
                occ = occ_at(a, here)
                for q in range(transfers):
                    sums[q] = sums[q] + occ * virt_at(slots[a * transfers + q], here)
            for q in range(transfers):
                chi[q, t, here, :] = sums[q]
            return inner

        lax.fori_loop(0, npts // SUB, piece, 0, unroll=2)

    def task(b, t):
        prev = (b + nk - 1) % nk
        for which, blk in ((0, prev), (1, b)):
            factor = factors(blk, t)
            for a in range(per):
                scale = factor[a:a + 1]
                vg[which * per + a] = virt_green(blk * per + a, scale)
                if which == 1:
                    og[a] = occ_green(blk * per + a, scale)
        add(t, [b * per + a for a in range(per)], prev * per, 2 * per,
            lambda a, here: og[a, here, :], lambda slot, here: vg[slot, here, :])

    hops = nr - 1
    total = nc * span
    edge = (c == 0) | (c == nc - 1)
    final = jnp.where(c == 0, nk - 2, 1)

    def prepare(t, inner):
        for first, blk in ((0, final - 1), (2 * per, final + 1)):
            factor = factors(blk, t)
            for a in range(per):
                scale = factor[a:a + 1]
                last_vg[t, first + a] = virt_green(blk * per + a, scale)
                if first > 0:
                    last_og[t, a] = occ_green(blk * per + a, scale)
        return inner

    def stream(a):
        m = final * per + a

        def one(t, inner):
            row = lax.broadcasted_iota(jnp.int32, (PAD, nall), 0)
            scale = jnp.sum(jnp.where(row == a, factors(final, t), 0.0), axis=0, keepdims=True)
            last_vg[t, per + a] = virt_green(m, scale)
            og[0] = occ_green(m, scale)
            add(t, [m], (final - 1) * per, 3 * per, lambda _, here: og[0, here, :], lambda slot, here: last_vg[t, slot, here, :])
            return inner

        lax.fori_loop(0, NTAU, one, 0)

    def close(t, inner):
        add(t, [(final + 1) * per + a for a in range(per)], (final - 1) * per, 3 * per,
            lambda a, here: last_og[t, a, here, :], lambda slot, here: last_vg[t, slot, here, :])
        return inner

    def work(n):
        v = n - hops - (span - 1)
        h, idx = v // span, v % span
        low, high = c - h, c + h
        rest = n - hops - (total - span + per - 1)

        @pl.when(edge & (rest == 0))
        def _():
            lax.fori_loop(0, NTAU, prepare, 0)

        @pl.when(edge & (rest > 0) & (rest <= per))
        def _():
            stream(rest - 1)

        @pl.when(edge & (rest == per))
        def _():
            lax.fori_loop(0, NTAU, close, 0)

        def one(w, inner):
            b_edge = jnp.where((h == 0) | (c > 0), 2 * low + 1 + w, 2 * high + w)
            ok_edge = (idx < NTAU) & ((h > 0) | (w == 0))
            b_mid = jnp.where(w == 0, 2 * low + 1 + idx % 2, 2 * high + idx % 2)
            ok_mid = jnp.where(w == 0, (low >= 0) & ((h > 0) | (idx % 2 == 0)), (high < nc) & (h > 0))
            ok = (v >= 0) & (h < nc - 1) & jnp.where(edge, ok_edge, ok_mid)
            wrap = w == 2
            ok = jnp.where(wrap, (rest >= 0) & (rest < NTAU), ok)
            b = jnp.where(wrap, 0, jnp.where(edge, b_edge, b_mid))
            t = jnp.where(wrap, rest, jnp.where(edge, idx, idx // 2))

            @pl.when(ok)
            def _():
                task(b, t)

            return inner

        lax.fori_loop(0, 3, one, 0)

    def clear(p, inner):
        q, t = p // NTAU, p % NTAU
        chi[q, t] = jnp.zeros((npts, ncol), jnp.float32)
        return inner

    def step(n, carry):
        @pl.when(n < total)
        def _():
            row_stage(n, True)

        @pl.when(n == 0)
        def _():
            lax.fori_loop(0, transfers * NTAU, clear, 0)

        for p, dist, device in ways:
            then = n - jnp.maximum(dist, 1)

            @pl.when((then >= 0) & (then < total))
            def _():
                col_stage(then, True, p, dist, device)

        work(n)
        return carry

    lax.fori_loop(0, total + hops, step, 0)

    def finish(n, carry):
        row_stage(n, False)
        for p, dist, device in ways:
            col_stage(n, False, p, dist, device)
        return carry

    lax.fori_loop(0, total, finish, 0)


def on_device(nk, nr, occ_orbitals, virt_orbitals, occ_gap, virt_gap, partner):
    per, npts, nocc = occ_orbitals.shape
    nv = virt_orbitals.shape[2]
    K, ncol, nall = nk * per, npts * nr // nk, nocc + nv
    transfers = partner.shape[0]
    gaps = jnp.pad(jnp.concatenate([occ_gap, virt_gap], axis=1), ((0, PAD - per), (0, 0)))
    dma = pltpu.SemaphoreType.DMA
    return pl.pallas_call(
        functools.partial(kernel, nk, nr, per),
        out_shape=jax.ShapeDtypeStruct((transfers, NTAU, npts, ncol), jnp.float32),
        in_specs=[pl.BlockSpec(memory_space=pl.ANY)] * 3 + [pl.BlockSpec(memory_space=pltpu.SMEM)],
        out_specs=pl.BlockSpec(memory_space=pltpu.VMEM),
        scratch_shapes=[
            pltpu.VMEM((K, npts, nall), jnp.bfloat16),
            pltpu.VMEM((K, ncol, nall), jnp.bfloat16),
            pltpu.VMEM((nk, PAD, nall), jnp.bfloat16),
            pltpu.VMEM((per, npts, ncol), jnp.float32),
            pltpu.VMEM((2 * per, npts, ncol), jnp.float32),
            pltpu.VMEM((NTAU, per, npts, ncol), jnp.float32),
            pltpu.VMEM((NTAU, 3 * per, npts, ncol), jnp.float32),
            dma((per, 2)), dma((K,)), dma((K,)), dma((K,)), dma((nk,)), dma((nk,)), dma((nk,)),
            dma((K, PIECES)), dma((K, PIECES)),
        ],
        compiler_params=pltpu.CompilerParams(
            collective_id=0, has_side_effects=True, vmem_limit_bytes=67043328),
    )(occ_orbitals, virt_orbitals, gaps, partner)


def solution(mesh):
    in_specs = (P("kpt", "row", None), P("kpt", "row", None), P("kpt", None), P("kpt", None), P())
    out_specs = P(None, None, "row", "kpt")
    return jax.shard_map(
        functools.partial(on_device, mesh.shape["kpt"], mesh.shape["row"]),
        mesh=mesh, in_specs=in_specs, out_specs=out_specs, check_vma=False,
    )
```

```python
import functools

import jax
import jax.numpy as jnp
from jax import lax
from jax.experimental import pallas as pl
from jax.experimental.pallas import tpu as pltpu
from jax.sharding import PartitionSpec as P

NTAU = 4
SUB = 32
PIECES = 4
BEHIND = 12


def kernel(nk, nr, per, occ_ref, virt_ref, occ_gap_ref, virt_gap_ref, partner_ref, chi, rows, cols, gaps, og, vg, last_og, last_vg,
           local_sem, gap_sem, row_recv, flow_send, sib_send, gap_recv, gap_flow, gap_sib, col_recv, col_send):
    K = nk * per
    npts, nocc = occ_ref.shape[1], occ_ref.shape[2]
    nall = rows.shape[2]
    ncol = cols.shape[1]
    width = ncol // PIECES
    transfers = partner_ref.shape[0]
    j = lax.axis_index("kpt")
    i = lax.axis_index("row")
    c, s = j // 2, j % 2
    nc = nk // 2
    cpr = nk // nr
    root = j // cpr
    off = (j % cpr) * ncol
    span = 2 * per

    def place(index):
        return jnp.where(index % 2 == 0, index // 2, nr - 1 - index // 2)

    def at_place(p):
        return jnp.where(p < nr // 2, 2 * p, 2 * (nr - 1 - p) + 1)

    me, top = place(i), place(root)
    ahead, behind = at_place((me + 1) % nr), at_place((me + nr - 1) % nr)
    dist_a, dist_b = (me - top + nr) % nr, (top - me + nr) % nr
    is_root = i == root
    up = s == 0
    has_next = jnp.where(up, c + 1 < nc, c > 0)
    has_prev = jnp.where(up, c > 0, c + 1 < nc)
    sib = j + 1 - 2 * s
    onward = j + 2 - 4 * s
    before = j - 2 + 4 * s

    def local_rows(a):
        m = j * per + a
        return (pltpu.make_async_copy(occ_ref.at[a], rows.at[m, :, pl.ds(0, nocc)], local_sem.at[a, 0]),
                pltpu.make_async_copy(virt_ref.at[a], rows.at[m, :, pl.ds(nocc, nall - nocc)], local_sem.at[a, 1]))

    local_gaps = (pltpu.make_async_copy(occ_gap_ref, gaps.at[j, :, pl.ds(0, nocc)], gap_sem.at[0]),
                  pltpu.make_async_copy(virt_gap_ref, gaps.at[j, :, pl.ds(nocc, nall - nocc)], gap_sem.at[1]))
    for copy in local_gaps:
        copy.start()
    for a in range(per):
        for copy in local_rows(a):
            copy.start()

    barrier = pltpu.get_barrier_semaphore()

    def greet(device):
        pl.semaphore_signal(barrier, inc=1, device_id=device, device_id_type=pl.DeviceIdType.MESH)

    greet((sib, i))
    greet((j, ahead))
    greet((j, behind))

    @pl.when(has_next)
    def _():
        greet((onward, i))

    @pl.when(has_prev)
    def _():
        greet((before, i))

    pl.semaphore_wait(barrier, 3 + has_next.astype(jnp.int32) + has_prev.astype(jnp.int32))

    def remote(src, dst, send, recv, device):
        return pltpu.make_async_remote_copy(src_ref=src, dst_ref=dst, send_sem=send, recv_sem=recv,
                                            device_id=device, device_id_type=pl.DeviceIdType.MESH)

    def row_flow(m):
        return remote(rows.at[m], rows.at[m], flow_send.at[m], row_recv.at[m], (onward, i))

    def row_sib(m):
        return remote(rows.at[m], rows.at[m], sib_send.at[m], row_recv.at[m], (sib, i))

    def gap_on(b):
        return remote(gaps.at[b], gaps.at[b], gap_flow.at[b], gap_recv.at[b], (onward, i))

    def gap_over(b):
        return remote(gaps.at[b], gaps.at[b], gap_sib.at[b], gap_recv.at[b], (sib, i))

    def part(p):
        return pl.ds(p * width, width)

    def source(m, p):
        return rows.at[m, pl.ds(pl.multiple_of(off + p * width, width), width)]

    def col_copy(m, p, device, from_root):
        src = source(m, p) if from_root else cols.at[m, part(p)]
        return remote(src, cols.at[m, part(p)], col_send.at[m, p], col_recv.at[m, p], (j, device))

    def root_copy(m, p):
        return pltpu.make_async_copy(source(m, p), cols.at[m, part(p)], col_recv.at[m, p])

    def wait_row(m):
        pltpu.make_async_copy(rows.at[m], rows.at[m], row_recv.at[m]).wait()

    def wait_gap(b):
        pltpu.make_async_copy(gaps.at[b], gaps.at[b], gap_recv.at[b]).wait()

    def wait_col(m, p):
        pltpu.make_async_copy(cols.at[m, part(p)], cols.at[m, part(p)], col_recv.at[m, p]).wait()

    ways = tuple((p, (dist_a, dist_b)[p % 2], (ahead, behind)[p % 2]) for p in range(PIECES))

    def root_send(m, start):
        @pl.when(is_root)
        def _():
            for p, _, device in ways:
                copy = col_copy(m, p, device, True)
                copy.start() if start else copy.wait_send()
                if start:
                    root_copy(m, p).start()

    def arrivals(n):
        h, idx = n // span, n % span
        low, high = c - h, c + h
        first = low * span + idx
        second = high * span + (idx + per) % span
        flow_ok = jnp.where(up, low >= 0, high < nc)
        other_ok = (h > 0) & jnp.where(up, high < nc, low >= 0)
        return h, idx, jnp.where(up, first, second), flow_ok, jnp.where(up, second, first), other_ok

    def row_stage(n, start):
        h, idx, fm, flow_ok, om, other_ok = arrivals(n)
        own = (h == 0) & (idx < per)
        lead = idx % per == 0

        def go(copy):
            copy.start() if start else copy.wait_send()

        @pl.when(flow_ok)
        def _():
            if start:
                @pl.when(own)
                def _():
                    for copy in local_rows(idx % per):
                        copy.wait()

                    @pl.when(lead)
                    def _():
                        for copy in local_gaps:
                            copy.wait()

                @pl.when(jnp.logical_not(own))
                def _():
                    wait_row(fm)

                    @pl.when(lead)
                    def _():
                        wait_gap(fm // per)

            @pl.when(has_next)
            def _():
                go(row_flow(fm))

                @pl.when(lead)
                def _():
                    go(gap_on(fm // per))

            @pl.when((h > 0) | own)
            def _():
                go(row_sib(fm))

                @pl.when(lead)
                def _():
                    go(gap_over(fm // per))

            root_send(fm, start)

        @pl.when(other_ok)
        def _():
            if start:
                wait_row(om)

                @pl.when(lead)
                def _():
                    wait_gap(om // per)
            root_send(om, start)

    def col_stage(n, start, p, dist, device):
        _, _, fm, flow_ok, om, other_ok = arrivals(n)
        for m, ok in ((fm, flow_ok), (om, other_ok)):
            @pl.when(ok)
            def _():
                if start:
                    wait_col(m, p)

                @pl.when((dist > 0) & (dist < nr - 1))
                def _():
                    copy = col_copy(m, p, device, False)
                    copy.start() if start else copy.wait_send()

    contract = (((1,), (1,)), ((), ()))

    def factors(b, t):
        moment = jnp.where(t == 0, 0.25, jnp.where(t == 1, 0.5, jnp.where(t == 2, 1.0, 2.0))).astype(jnp.float32)
        return jnp.exp(-gaps[b].astype(jnp.float32) * moment)

    def product(k, scale, low, size):
        panel = (rows[k, :, pl.ds(low, size)].astype(jnp.float32) * scale[:, low:low + size]).astype(jnp.bfloat16)
        return lax.dot_general(panel, cols[k, :, pl.ds(low, size)], contract, preferred_element_type=jnp.float32)

    def occ_green(k, scale):
        return product(k, scale, 0, nocc)

    def virt_green(k, scale):
        return product(k, scale, nocc, nall - nocc)

    def add(t, ks, base, held, occ_at, virt_at):
        slots = []
        for k in ks:
            for q in range(transfers):
                d = partner_ref[q, k] - base
                slots.append(jnp.minimum(jnp.where(d < 0, d + K, d), held - 1))

        def piece(p, inner):
            here = pl.ds(pl.multiple_of(p * SUB, SUB), SUB)
            sums = [chi[q, t, here, :] for q in range(transfers)]
            for a in range(len(ks)):
                occ = occ_at(a, here)
                for q in range(transfers):
                    sums[q] = sums[q] + occ * virt_at(slots[a * transfers + q], here)
            for q in range(transfers):
                chi[q, t, here, :] = sums[q]
            return inner

        lax.fori_loop(0, npts // SUB, piece, 0, unroll=2)

    def task(b, t):
        prev = (b + nk - 1) % nk
        for which, blk in ((0, prev), (1, b)):
            factor = factors(blk, t)
            for a in range(per):
                scale = factor[a:a + 1]
                vg[which * per + a] = virt_green(blk * per + a, scale)
                if which == 1:
                    og[a] = occ_green(blk * per + a, scale)
        add(t, [b * per + a for a in range(per)], prev * per, 2 * per,
            lambda a, here: og[a, here, :], lambda slot, here: vg[slot, here, :])

    hops = nr - 1
    total = nc * span
    edge = (c == 0) | (c == nc - 1)
    final = jnp.where(c == 0, nk - 2, 1)

    def prepare(t, after):
        blk = jnp.where(after, final + 1, final - 1)
        first = jnp.where(after, 2 * per, 0)
        factor = factors(blk, t)
        for a in range(per):
            last_vg[t, first + a] = virt_green(blk * per + a, factor[a:a + 1])

        @pl.when(after)
        def _():
            for a in range(per):
                last_og[t, a] = occ_green(blk * per + a, factor[a:a + 1])

    def stream(a):
        m = final * per + a

        def one(t, inner):
            row = lax.broadcasted_iota(jnp.int32, (per, nall), 0)
            scale = jnp.sum(jnp.where(row == a, factors(final, t), 0.0), axis=0, keepdims=True)
            last_vg[t, per + a] = virt_green(m, scale)
            og[0] = occ_green(m, scale)
            add(t, [m], (final - 1) * per, 3 * per, lambda _, here: og[0, here, :], lambda slot, here: last_vg[t, slot, here, :])
            return inner

        lax.fori_loop(0, NTAU, one, 0)

    def close(t, inner):
        add(t, [(final + 1) * per + a for a in range(per)], (final - 1) * per, 3 * per,
            lambda a, here: last_og[t, a, here, :], lambda slot, here: last_vg[t, slot, here, :])
        return inner

    def work(n):
        v = n - hops - (span - 1)
        h, idx = v // span, v % span
        low, high = c - h, c + h
        rest = n - hops - (total - span + per - 1)

        early = rest + span

        def ready(t, inner):
            prepare(jnp.where(rest == 0, t, early), jnp.where(rest == 0, c == 0, c > 0))
            return inner

        @pl.when(edge & ((rest == 0) | ((early >= 0) & (early < NTAU))))
        def _():
            lax.fori_loop(0, jnp.where(rest == 0, NTAU, 1), ready, 0)

        @pl.when(edge & (rest > 0) & (rest <= per))
        def _():
            stream(rest - 1)

        @pl.when(edge & (rest == per))
        def _():
            lax.fori_loop(0, NTAU, close, 0)

        def one(w, inner):
            b_edge = jnp.where((h == 0) | (c > 0), 2 * low + 1 + w, 2 * high + w)
            ok_edge = (idx < NTAU) & ((h > 0) | (w == 0))
            b_mid = jnp.where(w == 0, 2 * low + 1 + idx % 2, 2 * high + idx % 2)
            ok_mid = jnp.where(w == 0, (low >= 0) & ((h > 0) | (idx % 2 == 0)), (high < nc) & (h > 0))
            ok = (v >= 0) & (h < nc - 1) & jnp.where(edge, ok_edge, ok_mid)
            wrap = w == 2
            ok = jnp.where(wrap, (rest >= 0) & (rest < NTAU), ok)
            b = jnp.where(wrap, 0, jnp.where(edge, b_edge, b_mid))
            t = jnp.where(wrap, rest, jnp.where(edge, idx, idx // 2))

            @pl.when(ok)
            def _():
                task(b, t)

            return inner

        lax.fori_loop(0, 3, one, 0)

    def clear(p, inner):
        q, t = p // NTAU, p % NTAU
        chi[q, t] = jnp.zeros((npts, ncol), jnp.float32)
        return inner

    def sent(n):
        row_stage(n, False)
        for p, dist, device in ways:
            col_stage(n, False, p, dist, device)

    def step(n, carry):
        @pl.when(n < total)
        def _():
            row_stage(n, True)

        @pl.when(n == 0)
        def _():
            lax.fori_loop(0, transfers * NTAU, clear, 0)

        for p, dist, device in ways:
            then = n - jnp.maximum(dist, 1)

            @pl.when((then >= 0) & (then < total))
            def _():
                col_stage(then, True, p, dist, device)

        @pl.when((n >= BEHIND) & (n < total))
        def _():
            sent(n - BEHIND)

        work(n)
        return carry

    lax.fori_loop(0, total + hops, step, 0)

    def finish(n, carry):
        sent(n)
        return carry

    lax.fori_loop(total - BEHIND, total, finish, 0)


def on_device(nk, nr, occ_orbitals, virt_orbitals, occ_gap, virt_gap, partner):
    per, npts, nocc = occ_orbitals.shape
    nv = virt_orbitals.shape[2]
    K, ncol, nall = nk * per, npts * nr // nk, nocc + nv
    transfers = partner.shape[0]
    dma = pltpu.SemaphoreType.DMA
    return pl.pallas_call(
        functools.partial(kernel, nk, nr, per),
        out_shape=pltpu.VMEM((transfers, NTAU, npts, ncol), jnp.float32),
        in_specs=[pl.BlockSpec(memory_space=pl.ANY)] * 4 + [pl.BlockSpec(memory_space=pltpu.SMEM)],
        out_specs=pl.BlockSpec(memory_space=pltpu.VMEM),
        scratch_shapes=[
            pltpu.VMEM((K, npts, nall), jnp.bfloat16),
            pltpu.VMEM((K, ncol, nall), jnp.bfloat16),
            pltpu.VMEM((nk, per, nall), jnp.bfloat16),
            pltpu.VMEM((per, npts, ncol), jnp.float32),
            pltpu.VMEM((2 * per, npts, ncol), jnp.float32),
            pltpu.VMEM((NTAU, per, npts, ncol), jnp.float32),
            pltpu.VMEM((NTAU, 3 * per, npts, ncol), jnp.float32),
            dma((per, 2)), dma((2,)), dma((K,)), dma((K,)), dma((K,)), dma((nk,)), dma((nk,)), dma((nk,)),
            dma((K, PIECES)), dma((K, PIECES)),
        ],
        compiler_params=pltpu.CompilerParams(
            collective_id=0, has_side_effects=True, vmem_limit_bytes=57 * 2**20),
    )(occ_orbitals, virt_orbitals, occ_gap, virt_gap, partner)


def solution(mesh):
    in_specs = (P("kpt", "row", None), P("kpt", "row", None), P("kpt", None), P("kpt", None), P())
    out_specs = P(None, None, "row", "kpt")
    return jax.shard_map(
        functools.partial(on_device, mesh.shape["kpt"], mesh.shape["row"]),
        mesh=mesh, in_specs=in_specs, out_specs=out_specs, check_vma=False,
    )
```

```python
import functools

import jax
import jax.numpy as jnp
from jax import lax
from jax.experimental import pallas as pl
from jax.experimental.pallas import tpu as pltpu
from jax.sharding import PartitionSpec as P

NTAU = 4
SUB = 32
PIECES = 4
BEHIND = 12


def kernel(nk, nr, per, occ_ref, virt_ref, occ_gap_ref, virt_gap_ref, partner_ref, chi, rows, cols, gaps, og, vg, last_og, last_vg,
           local_sem, gap_sem, row_recv, flow_send, sib_send, gap_recv, gap_flow, gap_sib, col_recv, col_send):
    K = nk * per
    npts, nocc = occ_ref.shape[1], occ_ref.shape[2]
    nall = rows.shape[2]
    ncol = cols.shape[1]
    width = ncol // PIECES
    transfers = partner_ref.shape[0]
    j = lax.axis_index("kpt")
    i = lax.axis_index("row")
    c, s = j // 2, j % 2
    nc = nk // 2
    cpr = nk // nr
    root = j // cpr
    off = (j % cpr) * ncol
    span = 2 * per

    def place(index):
        return jnp.where(index % 2 == 0, index // 2, nr - 1 - index // 2)

    def at_place(p):
        return jnp.where(p < nr // 2, 2 * p, 2 * (nr - 1 - p) + 1)

    me, top = place(i), place(root)
    ahead, behind = at_place((me + 1) % nr), at_place((me + nr - 1) % nr)
    dist_a, dist_b = (me - top + nr) % nr, (top - me + nr) % nr
    is_root = i == root
    up = s == 0
    has_next = jnp.where(up, c + 1 < nc, c > 0)
    has_prev = jnp.where(up, c > 0, c + 1 < nc)
    sib = j + 1 - 2 * s
    onward = j + 2 - 4 * s
    before = j - 2 + 4 * s

    def local_rows(a):
        m = j * per + a
        return (pltpu.make_async_copy(occ_ref.at[a], rows.at[m, :, pl.ds(0, nocc)], local_sem.at[a, 0]),
                pltpu.make_async_copy(virt_ref.at[a], rows.at[m, :, pl.ds(nocc, nall - nocc)], local_sem.at[a, 1]))

    local_gaps = (pltpu.make_async_copy(occ_gap_ref, gaps.at[j, :, pl.ds(0, nocc)], gap_sem.at[0]),
                  pltpu.make_async_copy(virt_gap_ref, gaps.at[j, :, pl.ds(nocc, nall - nocc)], gap_sem.at[1]))
    for copy in local_gaps:
        copy.start()
    for a in range(per):
        for copy in local_rows(a):
            copy.start()

    barrier = pltpu.get_barrier_semaphore()

    def greet(device):
        pl.semaphore_signal(barrier, inc=1, device_id=device, device_id_type=pl.DeviceIdType.MESH)

    greet((sib, i))
    greet((j, ahead))
    greet((j, behind))

    @pl.when(has_next)
    def _():
        greet((onward, i))

    @pl.when(has_prev)
    def _():
        greet((before, i))

    pl.semaphore_wait(barrier, 3 + has_next.astype(jnp.int32) + has_prev.astype(jnp.int32))

    def remote(src, dst, send, recv, device):
        return pltpu.make_async_remote_copy(src_ref=src, dst_ref=dst, send_sem=send, recv_sem=recv,
                                            device_id=device, device_id_type=pl.DeviceIdType.MESH)

    def row_flow(m):
        return remote(rows.at[m], rows.at[m], flow_send.at[m], row_recv.at[m], (onward, i))

    def row_sib(m):
        return remote(rows.at[m], rows.at[m], sib_send.at[m], row_recv.at[m], (sib, i))

    def gap_on(b):
        return remote(gaps.at[b], gaps.at[b], gap_flow.at[b], gap_recv.at[b], (onward, i))

    def gap_over(b):
        return remote(gaps.at[b], gaps.at[b], gap_sib.at[b], gap_recv.at[b], (sib, i))

    def part(p):
        return pl.ds(p * width, width)

    def source(m, p):
        return rows.at[m, pl.ds(pl.multiple_of(off + p * width, width), width)]

    def col_copy(m, p, device, from_root):
        src = source(m, p) if from_root else cols.at[m, part(p)]
        return remote(src, cols.at[m, part(p)], col_send.at[m, p], col_recv.at[m, p], (j, device))

    def root_copy(m, p):
        return pltpu.make_async_copy(source(m, p), cols.at[m, part(p)], col_recv.at[m, p])

    def wait_row(m):
        pltpu.make_async_copy(rows.at[m], rows.at[m], row_recv.at[m]).wait()

    def wait_gap(b):
        pltpu.make_async_copy(gaps.at[b], gaps.at[b], gap_recv.at[b]).wait()

    def wait_col(m, p):
        pltpu.make_async_copy(cols.at[m, part(p)], cols.at[m, part(p)], col_recv.at[m, p]).wait()

    ways = tuple((p, (dist_a, dist_b)[p % 2], (ahead, behind)[p % 2]) for p in range(PIECES))

    def root_send(m, start):
        @pl.when(is_root)
        def _():
            for p, _, device in ways:
                copy = col_copy(m, p, device, True)
                copy.start() if start else copy.wait_send()
                if start:
                    root_copy(m, p).start()

    def arrivals(n):
        h, idx = lax.div(n, span), lax.rem(n, span)
        low, high = c - h, c + h
        first = low * span + idx
        second = high * span + lax.rem(idx + per, span)
        flow_ok = jnp.where(up, low >= 0, high < nc)
        other_ok = (h > 0) & jnp.where(up, high < nc, low >= 0)
        return h, idx, jnp.where(up, first, second), flow_ok, jnp.where(up, second, first), other_ok

    def row_stage(came, start):
        h, idx, fm, flow_ok, om, other_ok = came
        own = (h == 0) & (idx < per)
        lead = lax.rem(idx, per) == 0

        def go(copy):
            copy.start() if start else copy.wait_send()

        @pl.when(flow_ok)
        def _():
            if start:
                @pl.when(own)
                def _():
                    for copy in local_rows(lax.rem(idx, per)):
                        copy.wait()

                    @pl.when(lead)
                    def _():
                        for copy in local_gaps:
                            copy.wait()

                @pl.when(jnp.logical_not(own))
                def _():
                    wait_row(fm)

                    @pl.when(lead)
                    def _():
                        wait_gap(lax.div(fm, per))

            @pl.when(has_next)
            def _():
                go(row_flow(fm))

                @pl.when(lead)
                def _():
                    go(gap_on(lax.div(fm, per)))

            @pl.when((h > 0) | own)
            def _():
                go(row_sib(fm))

                @pl.when(lead)
                def _():
                    go(gap_over(lax.div(fm, per)))

            root_send(fm, start)

        @pl.when(other_ok)
        def _():
            if start:
                wait_row(om)

                @pl.when(lead)
                def _():
                    wait_gap(lax.div(om, per))
            root_send(om, start)

    def col_stage(came, start, p, dist, device):
        _, _, fm, flow_ok, om, other_ok = came
        for m, ok in ((fm, flow_ok), (om, other_ok)):
            @pl.when(ok)
            def _():
                if start:
                    wait_col(m, p)

                @pl.when((dist > 0) & (dist < nr - 1))
                def _():
                    copy = col_copy(m, p, device, False)
                    copy.start() if start else copy.wait_send()

    contract = (((1,), (1,)), ((), ()))

    def factors(b, t):
        moment = jnp.where(t == 0, 0.25, jnp.where(t == 1, 0.5, jnp.where(t == 2, 1.0, 2.0))).astype(jnp.float32)
        return jnp.exp(-gaps[b].astype(jnp.float32) * moment)

    def product(k, scale, low, size):
        panel = (rows[k, :, pl.ds(low, size)].astype(jnp.float32) * scale[:, low:low + size]).astype(jnp.bfloat16)
        return lax.dot_general(panel, cols[k, :, pl.ds(low, size)], contract, preferred_element_type=jnp.float32)

    def occ_green(k, scale):
        return product(k, scale, 0, nocc)

    def virt_green(k, scale):
        return product(k, scale, nocc, nall - nocc)

    def add(t, ks, base, held, occ_at, virt_at):
        slots = []
        for k in ks:
            for q in range(transfers):
                d = partner_ref[q, k] - base
                slots.append(jnp.minimum(jnp.where(d < 0, d + K, d), held - 1))

        def piece(p, inner):
            here = pl.ds(pl.multiple_of(p * SUB, SUB), SUB)
            sums = [chi[q, t, here, :] for q in range(transfers)]
            for a in range(len(ks)):
                occ = occ_at(a, here)
                for q in range(transfers):
                    sums[q] = sums[q] + occ * virt_at(slots[a * transfers + q], here)
            for q in range(transfers):
                chi[q, t, here, :] = sums[q]
            return inner

        lax.fori_loop(0, npts // SUB, piece, 0, unroll=2)

    def task(b, t):
        prev = (b + nk - 1) % nk
        for which, blk in ((0, prev), (1, b)):
            factor = factors(blk, t)
            for a in range(per):
                scale = factor[a:a + 1]
                vg[which * per + a] = virt_green(blk * per + a, scale)
                if which == 1:
                    og[a] = occ_green(blk * per + a, scale)
        add(t, [b * per + a for a in range(per)], prev * per, 2 * per,
            lambda a, here: og[a, here, :], lambda slot, here: vg[slot, here, :])

    total = nc * span
    edge = (c == 0) | (c == nc - 1)
    lag = jnp.where(edge, 1, 2)
    hops = lag * jnp.maximum(jnp.maximum(dist_a, dist_b), 1)
    final = jnp.where(c == 0, nk - 2, 1)

    def prepare(t, after):
        blk = jnp.where(after, final + 1, final - 1)
        first = jnp.where(after, 2 * per, 0)
        factor = factors(blk, t)
        for a in range(per):
            last_vg[t, first + a] = virt_green(blk * per + a, factor[a:a + 1])

        @pl.when(after)
        def _():
            for a in range(per):
                last_og[t, a] = occ_green(blk * per + a, factor[a:a + 1])

    def stream(a):
        m = final * per + a

        def one(t, inner):
            row = lax.broadcasted_iota(jnp.int32, (per, nall), 0)
            scale = jnp.sum(jnp.where(row == a, factors(final, t), 0.0), axis=0, keepdims=True)
            last_vg[t, per + a] = virt_green(m, scale)
            og[0] = occ_green(m, scale)
            add(t, [m], (final - 1) * per, 3 * per, lambda _, here: og[0, here, :], lambda slot, here: last_vg[t, slot, here, :])
            return inner

        lax.fori_loop(0, NTAU, one, 0)

    def close(t, inner):
        add(t, [(final + 1) * per + a for a in range(per)], (final - 1) * per, 3 * per,
            lambda a, here: last_og[t, a, here, :], lambda slot, here: last_vg[t, slot, here, :])
        return inner

    def work(n):
        v = n - hops - (span - 1)
        h, idx = lax.div(jnp.maximum(v, 0), span), lax.rem(jnp.maximum(v, 0), span)
        low, high = c - h, c + h
        rest = n - hops - (total - span + per - 1)

        early = rest + span
        at_once = (rest == 0) & (c > 0)
        each = jnp.where(rest < 0, early, rest)

        def ready(t, inner):
            prepare(jnp.where(at_once, t, each), jnp.where(rest < 0, c > 0, c == 0))
            return inner

        @pl.when(edge & (at_once | ((each >= 0) & (each < NTAU) & ((rest < 0) | (c == 0)))))
        def _():
            lax.fori_loop(0, jnp.where(at_once, NTAU, 1), ready, 0)

        @pl.when(edge & (rest > 0) & (rest <= per))
        def _():
            stream(rest - 1)

        @pl.when(edge & (rest == per))
        def _():
            lax.fori_loop(0, NTAU, close, 0)

        def one(w, inner):
            b_edge = jnp.where((h == 0) | (c > 0), 2 * low + 1 + w, 2 * high + w)
            ok_edge = (idx < NTAU) & ((h > 0) | (w == 0))
            b_mid = jnp.where(w == 0, 2 * low + 1 + idx % 2, 2 * high + idx % 2)
            ok_mid = jnp.where(w == 0, (low >= 0) & ((h > 0) | (idx % 2 == 0)), (high < nc) & (h > 0))
            ok = (v >= 0) & (h < nc - 1) & jnp.where(edge, ok_edge, ok_mid)
            wrap = w == 2
            ok = jnp.where(wrap, (rest >= 0) & (rest < NTAU), ok)
            b = jnp.where(wrap, 0, jnp.where(edge, b_edge, b_mid))
            t = jnp.where(wrap, rest, jnp.where(edge, idx, idx // 2))

            @pl.when(ok)
            def _():
                task(b, t)

            return inner

        lax.fori_loop(0, 3, one, 0)

    def clear(p, inner):
        q, t = p // NTAU, p % NTAU
        chi[q, t] = jnp.zeros((npts, ncol), jnp.float32)
        return inner

    def sent(n):
        came = arrivals(n)
        row_stage(came, False)
        for p, dist, device in ways:
            col_stage(came, False, p, dist, device)

    def step(n, carry):
        @pl.when(n < total)
        def _():
            row_stage(arrivals(n), True)

        @pl.when(n == 0)
        def _():
            lax.fori_loop(0, transfers * NTAU, clear, 0)

        thens = [n - lag * jnp.maximum(dist, 1) for dist in (dist_a, dist_b)]
        cames = [arrivals(jnp.maximum(then, 0)) for then in thens]
        for p, dist, device in ways:
            then = thens[p % 2]

            @pl.when((then >= 0) & (then < total))
            def _():
                col_stage(cames[p % 2], True, p, dist, device)

        @pl.when((n >= BEHIND) & (n < total))
        def _():
            sent(n - BEHIND)

        work(n)
        return carry

    lax.fori_loop(0, total + hops, step, 0)

    def finish(n, carry):
        sent(n)
        return carry

    lax.fori_loop(total - BEHIND, total, finish, 0)


def on_device(nk, nr, occ_orbitals, virt_orbitals, occ_gap, virt_gap, partner):
    per, npts, nocc = occ_orbitals.shape
    nv = virt_orbitals.shape[2]
    K, ncol, nall = nk * per, npts * nr // nk, nocc + nv
    transfers = partner.shape[0]
    dma = pltpu.SemaphoreType.DMA
    return pl.pallas_call(
        functools.partial(kernel, nk, nr, per),
        out_shape=pltpu.VMEM((transfers, NTAU, npts, ncol), jnp.float32),
        in_specs=[pl.BlockSpec(memory_space=pl.ANY)] * 4 + [pl.BlockSpec(memory_space=pltpu.SMEM)],
        out_specs=pl.BlockSpec(memory_space=pltpu.VMEM),
        scratch_shapes=[
            pltpu.VMEM((K, npts, nall), jnp.bfloat16),
            pltpu.VMEM((K, ncol, nall), jnp.bfloat16),
            pltpu.VMEM((nk, per, nall), jnp.bfloat16),
            pltpu.VMEM((per, npts, ncol), jnp.float32),
            pltpu.VMEM((2 * per, npts, ncol), jnp.float32),
            pltpu.VMEM((NTAU, per, npts, ncol), jnp.float32),
            pltpu.VMEM((NTAU, 3 * per, npts, ncol), jnp.float32),
            dma((per, 2)), dma((2,)), dma((K,)), dma((K,)), dma((K,)), dma((nk,)), dma((nk,)), dma((nk,)),
            dma((K, PIECES)), dma((K, PIECES)),
        ],
        compiler_params=pltpu.CompilerParams(
            collective_id=0, has_side_effects=True, vmem_limit_bytes=57 * 2**20),
    )(occ_orbitals, virt_orbitals, occ_gap, virt_gap, partner)


def solution(mesh):
    in_specs = (P("kpt", "row", None), P("kpt", "row", None), P("kpt", None), P("kpt", None), P())
    out_specs = P(None, None, "row", "kpt")
    return jax.shard_map(
        functools.partial(on_device, mesh.shape["kpt"], mesh.shape["row"]),
        mesh=mesh, in_specs=in_specs, out_specs=out_specs, check_vma=False,
    )
```

```python
import functools

import jax
import jax.numpy as jnp
from jax import lax
from jax.experimental import pallas as pl
from jax.experimental.pallas import tpu as pltpu
from jax.sharding import PartitionSpec as P

NTAU = 4
SUB = 32
PIECES = 4
BEHIND = 12


def kernel(nk, nr, per, occ_ref, virt_ref, occ_gap_ref, virt_gap_ref, partner_ref, chi, rows, cols, gaps, og, vg, last_og, last_vg,
           local_sem, gap_sem, row_recv, flow_send, sib_send, gap_recv, gap_flow, gap_sib, col_recv, col_send):
    K = nk * per
    npts, nocc = occ_ref.shape[1], occ_ref.shape[2]
    nall = rows.shape[2]
    ncol = cols.shape[1]
    width = ncol // PIECES
    transfers = partner_ref.shape[0]
    j = lax.axis_index("kpt")
    i = lax.axis_index("row")
    c, s = j // 2, j % 2
    nc = nk // 2
    cpr = nk // nr
    root = j // cpr
    off = (j % cpr) * ncol
    span = 2 * per

    def place(index):
        return jnp.where(index % 2 == 0, index // 2, nr - 1 - index // 2)

    def at_place(p):
        return jnp.where(p < nr // 2, 2 * p, 2 * (nr - 1 - p) + 1)

    me, top = place(i), place(root)
    ahead, behind = at_place((me + 1) % nr), at_place((me + nr - 1) % nr)
    dist_a, dist_b = (me - top + nr) % nr, (top - me + nr) % nr
    is_root = i == root
    up = s == 0
    has_next = jnp.where(up, c + 1 < nc, c > 0)
    has_prev = jnp.where(up, c > 0, c + 1 < nc)
    sib = j + 1 - 2 * s
    onward = j + 2 - 4 * s
    before = j - 2 + 4 * s

    def local_rows(a):
        m = j * per + a
        return (pltpu.make_async_copy(occ_ref.at[a], rows.at[m, :, pl.ds(0, nocc)], local_sem.at[a, 0]),
                pltpu.make_async_copy(virt_ref.at[a], rows.at[m, :, pl.ds(nocc, nall - nocc)], local_sem.at[a, 1]))

    local_gaps = (pltpu.make_async_copy(occ_gap_ref, gaps.at[j, :, pl.ds(0, nocc)], gap_sem.at[0]),
                  pltpu.make_async_copy(virt_gap_ref, gaps.at[j, :, pl.ds(nocc, nall - nocc)], gap_sem.at[1]))
    for copy in local_gaps:
        copy.start()
    for a in range(per):
        for copy in local_rows(a):
            copy.start()

    barrier = pltpu.get_barrier_semaphore()

    def greet(device):
        pl.semaphore_signal(barrier, inc=1, device_id=device, device_id_type=pl.DeviceIdType.MESH)

    greet((sib, i))
    greet((j, ahead))
    greet((j, behind))

    @pl.when(has_next)
    def _():
        greet((onward, i))

    @pl.when(has_prev)
    def _():
        greet((before, i))

    pl.semaphore_wait(barrier, 3 + has_next.astype(jnp.int32) + has_prev.astype(jnp.int32))

    def remote(src, dst, send, recv, device):
        return pltpu.make_async_remote_copy(src_ref=src, dst_ref=dst, send_sem=send, recv_sem=recv,
                                            device_id=device, device_id_type=pl.DeviceIdType.MESH)

    def row_flow(m):
        return remote(rows.at[m], rows.at[m], flow_send.at[m], row_recv.at[m], (onward, i))

    def row_sib(m):
        return remote(rows.at[m], rows.at[m], sib_send.at[m], row_recv.at[m], (sib, i))

    def gap_on(b):
        return remote(gaps.at[b], gaps.at[b], gap_flow.at[b], gap_recv.at[b], (onward, i))

    def gap_over(b):
        return remote(gaps.at[b], gaps.at[b], gap_sib.at[b], gap_recv.at[b], (sib, i))

    def part(p):
        return pl.ds(p * width, width)

    def source(m, p):
        return rows.at[m, pl.ds(pl.multiple_of(off + p * width, width), width)]

    def col_copy(m, p, device, from_root):
        src = source(m, p) if from_root else cols.at[m, part(p)]
        return remote(src, cols.at[m, part(p)], col_send.at[m, p], col_recv.at[m, p], (j, device))

    def root_copy(m, p):
        return pltpu.make_async_copy(source(m, p), cols.at[m, part(p)], col_recv.at[m, p])

    def wait_row(m):
        pltpu.make_async_copy(rows.at[m], rows.at[m], row_recv.at[m]).wait()

    def wait_gap(b):
        pltpu.make_async_copy(gaps.at[b], gaps.at[b], gap_recv.at[b]).wait()

    def wait_col(m, p):
        pltpu.make_async_copy(cols.at[m, part(p)], cols.at[m, part(p)], col_recv.at[m, p]).wait()

    ways = tuple((p, (dist_a, dist_b)[p % 2], (ahead, behind)[p % 2]) for p in range(PIECES))

    def root_send(m, start):
        @pl.when(is_root)
        def _():
            for p, _, device in ways:
                copy = col_copy(m, p, device, True)
                copy.start() if start else copy.wait_send()
                if start:
                    root_copy(m, p).start()

    def arrivals(n):
        h, idx = lax.div(n, span), lax.rem(n, span)
        low, high = c - h, c + h
        first = low * span + idx
        second = high * span + lax.rem(idx + per, span)
        flow_ok = jnp.where(up, low >= 0, high < nc)
        other_ok = (h > 0) & jnp.where(up, high < nc, low >= 0)
        return h, idx, jnp.where(up, first, second), flow_ok, jnp.where(up, second, first), other_ok

    def row_stage(came, start):
        h, idx, fm, flow_ok, om, other_ok = came
        own = (h == 0) & (idx < per)
        lead = lax.rem(idx, per) == 0

        def go(copy):
            copy.start() if start else copy.wait_send()

        @pl.when(flow_ok)
        def _():
            if start:
                @pl.when(own)
                def _():
                    for copy in local_rows(lax.rem(idx, per)):
                        copy.wait()

                    @pl.when(lead)
                    def _():
                        for copy in local_gaps:
                            copy.wait()

                @pl.when(jnp.logical_not(own))
                def _():
                    wait_row(fm)

                    @pl.when(lead)
                    def _():
                        wait_gap(lax.div(fm, per))

            @pl.when(has_next)
            def _():
                go(row_flow(fm))

                @pl.when(lead)
                def _():
                    go(gap_on(lax.div(fm, per)))

            @pl.when((h > 0) | own)
            def _():
                go(row_sib(fm))

                @pl.when(lead)
                def _():
                    go(gap_over(lax.div(fm, per)))

            root_send(fm, start)

        @pl.when(other_ok)
        def _():
            if start:
                wait_row(om)

                @pl.when(lead)
                def _():
                    wait_gap(lax.div(om, per))
            root_send(om, start)

    def col_stage(came, start, p, dist, device):
        _, _, fm, flow_ok, om, other_ok = came
        for m, ok in ((fm, flow_ok), (om, other_ok)):
            @pl.when(ok)
            def _():
                if start:
                    wait_col(m, p)

                @pl.when((dist > 0) & (dist < nr - 1))
                def _():
                    copy = col_copy(m, p, device, False)
                    copy.start() if start else copy.wait_send()

    contract = (((1,), (1,)), ((), ()))

    def factors(b, t):
        moment = jnp.where(t == 0, 0.25, jnp.where(t == 1, 0.5, jnp.where(t == 2, 1.0, 2.0))).astype(jnp.float32)
        return jnp.exp(-gaps[b].astype(jnp.float32) * moment)

    def product(k, scale, low, size):
        panel = (rows[k, :, pl.ds(low, size)].astype(jnp.float32) * scale[:, low:low + size]).astype(jnp.bfloat16)
        return lax.dot_general(panel, cols[k, :, pl.ds(low, size)], contract, preferred_element_type=jnp.float32)

    def occ_green(k, scale):
        return product(k, scale, 0, nocc)

    def virt_green(k, scale):
        return product(k, scale, nocc, nall - nocc)

    def add(t, ks, base, held, occ_at, virt_at):
        slots = []
        for k in ks:
            for q in range(transfers):
                d = partner_ref[q, k] - base
                slots.append(jnp.minimum(jnp.where(d < 0, d + K, d), held - 1))

        def piece(p, inner):
            here = pl.ds(pl.multiple_of(p * SUB, SUB), SUB)
            sums = [chi[q, t, here, :] for q in range(transfers)]
            for a in range(len(ks)):
                occ = occ_at(a, here)
                for q in range(transfers):
                    sums[q] = sums[q] + occ * virt_at(slots[a * transfers + q], here)
            for q in range(transfers):
                chi[q, t, here, :] = sums[q]
            return inner

        lax.fori_loop(0, npts // SUB, piece, 0, unroll=2)

    def task(b, t):
        prev = (b + nk - 1) % nk
        for which, blk in ((0, prev), (1, b)):
            factor = factors(blk, t)
            for a in range(per):
                scale = factor[a:a + 1]
                vg[which * per + a] = virt_green(blk * per + a, scale)
                if which == 1:
                    og[a] = occ_green(blk * per + a, scale)
        add(t, [b * per + a for a in range(per)], prev * per, 2 * per,
            lambda a, here: og[a, here, :], lambda slot, here: vg[slot, here, :])

    total = nc * span
    edge = (c == 0) | (c == nc - 1)
    lag = jnp.where(edge, 1, 2)
    hops = lag * jnp.maximum(jnp.maximum(dist_a, dist_b), 1)
    final = jnp.where(c == 0, nk - 2, 1)

    def prepare(t, after):
        blk = jnp.where(after, final + 1, final - 1)
        first = jnp.where(after, 2 * per, 0)
        factor = factors(blk, t)
        for a in range(per):
            last_vg[t, first + a] = virt_green(blk * per + a, factor[a:a + 1])

        @pl.when(after)
        def _():
            for a in range(per):
                last_og[t, a] = occ_green(blk * per + a, factor[a:a + 1])

    def stream(a):
        m = final * per + a

        def one(t, inner):
            row = lax.broadcasted_iota(jnp.int32, (per, nall), 0)
            scale = jnp.sum(jnp.where(row == a, factors(final, t), 0.0), axis=0, keepdims=True)
            last_vg[t, per + a] = virt_green(m, scale)
            og[0] = occ_green(m, scale)
            add(t, [m], (final - 1) * per, 3 * per, lambda _, here: og[0, here, :], lambda slot, here: last_vg[t, slot, here, :])
            return inner

        lax.fori_loop(0, NTAU, one, 0)

    def close(t, inner):
        add(t, [(final + 1) * per + a for a in range(per)], (final - 1) * per, 3 * per,
            lambda a, here: last_og[t, a, here, :], lambda slot, here: last_vg[t, slot, here, :])
        return inner

    def work(n):
        v = n - hops - (span - 1)
        h, idx = lax.div(jnp.maximum(v, 0), span), lax.rem(jnp.maximum(v, 0), span)
        low, high = c - h, c + h
        rest = n - hops - (total - span + per - 1)

        early = rest + span
        at_once = (rest == 0) & (c > 0)
        each = jnp.where(rest < 0, early, rest)

        def ready(t, inner):
            prepare(jnp.where(at_once, t, each), jnp.where(rest < 0, c > 0, c == 0))
            return inner

        @pl.when(edge & (at_once | ((each >= 0) & (each < NTAU) & ((rest < 0) | (c == 0)))))
        def _():
            lax.fori_loop(0, jnp.where(at_once, NTAU, 1), ready, 0)

        @pl.when(edge & (rest > 0) & (rest <= per))
        def _():
            stream(rest - 1)

        @pl.when(edge & (rest == per))
        def _():
            lax.fori_loop(0, NTAU, close, 0)

        def one(w, inner):
            b_edge = jnp.where((h == 0) | (c > 0), 2 * low + 1 + w, 2 * high + w)
            ok_edge = (idx < NTAU) & ((h > 0) | (w == 0))
            b_mid = jnp.where(w == 0, 2 * low + 1 + idx % 2, 2 * high + idx % 2)
            ok_mid = jnp.where(w == 0, (low >= 0) & ((h > 0) | (idx % 2 == 0)), (high < nc) & (h > 0))
            ok = (v >= 0) & (h < nc - 1) & jnp.where(edge, ok_edge, ok_mid)
            wrap = w >= 2
            turn = jnp.where(w == 3, 1, jnp.where(rest > 0, rest + 1, 0))
            ok = jnp.where(wrap, (rest >= 0) & (turn < NTAU) & ((w == 2) | (rest == 0)), ok)
            b = jnp.where(wrap, 0, jnp.where(edge, b_edge, b_mid))
            t = jnp.where(wrap, turn, jnp.where(edge, idx, idx // 2))

            @pl.when(ok)
            def _():
                task(b, t)

            return inner

        lax.fori_loop(0, 4, one, 0)

    def clear(p, inner):
        q, t = p // NTAU, p % NTAU
        chi[q, t] = jnp.zeros((npts, ncol), jnp.float32)
        return inner

    def sent(n):
        came = arrivals(n)
        row_stage(came, False)
        for p, dist, device in ways:
            col_stage(came, False, p, dist, device)

    def step(n, carry):
        @pl.when(n < total)
        def _():
            row_stage(arrivals(n), True)

        @pl.when(n == 0)
        def _():
            lax.fori_loop(0, transfers * NTAU, clear, 0)

        thens = [n - lag * jnp.maximum(dist, 1) for dist in (dist_a, dist_b)]
        cames = [arrivals(jnp.maximum(then, 0)) for then in thens]
        for p, dist, device in ways:
            then = thens[p % 2]

            @pl.when((then >= 0) & (then < total))
            def _():
                col_stage(cames[p % 2], True, p, dist, device)

        @pl.when((n >= BEHIND) & (n < total))
        def _():
            sent(n - BEHIND)

        work(n)
        return carry

    lax.fori_loop(0, total + hops, step, 0)

    def finish(n, carry):
        sent(n)
        return carry

    lax.fori_loop(total - BEHIND, total, finish, 0)


def on_device(nk, nr, occ_orbitals, virt_orbitals, occ_gap, virt_gap, partner):
    per, npts, nocc = occ_orbitals.shape
    nv = virt_orbitals.shape[2]
    K, ncol, nall = nk * per, npts * nr // nk, nocc + nv
    transfers = partner.shape[0]
    dma = pltpu.SemaphoreType.DMA
    return pl.pallas_call(
        functools.partial(kernel, nk, nr, per),
        out_shape=pltpu.VMEM((transfers, NTAU, npts, ncol), jnp.float32),
        in_specs=[pl.BlockSpec(memory_space=pl.ANY)] * 4 + [pl.BlockSpec(memory_space=pltpu.SMEM)],
        out_specs=pl.BlockSpec(memory_space=pltpu.VMEM),
        scratch_shapes=[
            pltpu.VMEM((K, npts, nall), jnp.bfloat16),
            pltpu.VMEM((K, ncol, nall), jnp.bfloat16),
            pltpu.VMEM((nk, per, nall), jnp.bfloat16),
            pltpu.VMEM((per, npts, ncol), jnp.float32),
            pltpu.VMEM((2 * per, npts, ncol), jnp.float32),
            pltpu.VMEM((NTAU, per, npts, ncol), jnp.float32),
            pltpu.VMEM((NTAU, 3 * per, npts, ncol), jnp.float32),
            dma((per, 2)), dma((2,)), dma((K,)), dma((K,)), dma((K,)), dma((nk,)), dma((nk,)), dma((nk,)),
            dma((K, PIECES)), dma((K, PIECES)),
        ],
        compiler_params=pltpu.CompilerParams(
            collective_id=0, has_side_effects=True, vmem_limit_bytes=57 * 2**20),
    )(occ_orbitals, virt_orbitals, occ_gap, virt_gap, partner)


def solution(mesh):
    in_specs = (P("kpt", "row", None), P("kpt", "row", None), P("kpt", None), P("kpt", None), P())
    out_specs = P(None, None, "row", "kpt")
    return jax.shard_map(
        functools.partial(on_device, mesh.shape["kpt"], mesh.shape["row"]),
        mesh=mesh, in_specs=in_specs, out_specs=out_specs, check_vma=False,
    )
```
